512 devices in a mesh: dp: 4 (over y), expert: 128 (over x, z, core).
Axes of the slice: x: 4, y: 4, z: 16, core: 2. Of those that a mesh axis runs over, the one named last changes fastest.
Arguments:
- slot_grads: bfloat16 [4, 128, 384, 2048], P('dp', 'expert'), may hold values from -0.23925781 to 0.23925781
- momentum: float32 [384, 64, 2048], P('expert', None, 'dp'), may hold values from -0.16 to 0.16
- master_weights: float32 [384, 64, 2048], P('expert', None, 'dp'), may hold values from -0.3125 to 0.3125
- current_slots: int32 [128, 1], replicated, may hold values from 0 to 63
- next_slots: int32 [128, 1], replicated, may hold values from 0 to 63
- live_counts: int32 [4, 128], P('dp', 'expert'), may hold values from 1 to 512
- route_index: int32 [4, 128, 4, 128], P('dp', 'expert'), may hold values from 0 to 127, each once within a row
- activations: bfloat16 [4, 128, 512, 384], P('dp', 'expert'), may hold values from -6 to 6
Outputs:
- new_momentum: float32 [384, 64, 2048], P('expert', None, 'dp')
- expert_out: bfloat16 [4, 128, 512, 2048], P('dp', 'expert')
The draws below stay inside these ranges and needn't reach their ends.
Inputs may be any that keep to these rules, and one draw needn't show every extreme that they name: `current_slots`: every expert is held by at least one slot. `next_slots`: every expert is held by at least one slot. `route_index`: each block of 128 indices names every row of its block once.
All inputs are finite; a program needn't handle non-finite values.
Results may differ from the reference program's by a relative error of at most 0.015.
Values may be sent and summed in bfloat16 or wider, within the bound.
A program may use at most 64 MiB of HBM per device.

```python
import jax
import jax.numpy as jnp
from jax import lax

D = 2048
FF_W = 384
QBLOCK = 128
RBLOCK = 128
ROWS = 512
EXPERTS = 64
SLOTS = 128
N_DP = 4


def set_ends(result, own_key, smallest, largest):
    extent = result.shape
    index_at = [jax.random.randint(jax.random.fold_in(own_key, axis), (), 0, extent[axis]) for axis in range(len(extent))]
    result = result.at[tuple(index_at)].set(smallest)
    longest = extent.index(max(extent))
    index_at[longest] = (index_at[longest] + 1) % extent[longest]
    return result.at[tuple(index_at)].set(largest)


def level_of(key, shape, shards, smallest, top_value):
    factor_of, own = 1.0, jax.random.fold_in(key, 6)
    for position, shards_of in shards:
        draws = jnp.exp(jax.random.uniform(jax.random.fold_in(own, position), (shards_of,), jnp.float32, smallest / len(shards), top_value / len(shards)))
        factor_of = factor_of * jnp.repeat(draws, shape[position] // shards_of).reshape([-1 if axis == position else 1 for axis in range(len(shape))])
    return factor_of


def distinct(key, rows, amount, top, lift):
    sequence = jax.random.permutation(jax.random.fold_in(key, 1), amount)
    boost = sequence
    for power in range(3):
        boost = boost * boost // amount
    boost = boost * lift // amount
    chance = jax.random.randint(jax.random.fold_in(key, 2), (rows, amount), 0, 4096) + boost
    fixed_rows = jax.random.permutation(jax.random.fold_in(key, 3), rows)[jnp.arange(amount) % rows]
    chance = jnp.where(jnp.arange(rows)[:, None] == fixed_rows[None, :], 1 << 14, chance)
    priority = chance * amount + jnp.arange(amount)
    return lax.top_k(priority.astype(jnp.int32), top)[1].astype(jnp.int32)


def gaussian(own_key, extent, width, limit, shards=(), kind=jnp.bfloat16):
    array = width * jax.random.normal(own_key, extent, jnp.float32)
    if shards:
        array = array * level_of(own_key, extent, shards, -0.22, 0.18)
    return jnp.clip(array, -limit, limit).astype(kind)


def setup_inputs(seed: int = 0) -> dict:
    splits = jax.random.split(jax.random.key(seed), 9)
    slot_grads = gaussian(splits[0], (N_DP, SLOTS, FF_W, D), 0.03, 0.23925781, ((0, 4), (1, 128)))
    momentum = gaussian(splits[1], (FF_W, EXPERTS, D), 0.02, 0.16, ((0, 128), (2, 4)), jnp.float32)
    master_weights = gaussian(splits[2], (FF_W, EXPERTS, D), FF_W ** -0.5, 0.3125, ((0, 128), (2, 4)), jnp.float32)
    current_slots = distinct(splits[3], SLOTS, EXPERTS, 1, 256)
    next_slots = distinct(splits[4], SLOTS, EXPERTS, 1, 256)
    live_counts = set_ends(jax.random.randint(splits[5], (N_DP, SLOTS), 1, ROWS + 1), jax.random.fold_in(splits[5], 1), 1, ROWS).astype(jnp.int32)
    route_index = jax.vmap(lambda own: jax.random.permutation(own, RBLOCK))(jax.random.split(splits[6], N_DP * SLOTS * (ROWS // RBLOCK))).reshape((N_DP, SLOTS, ROWS // RBLOCK, RBLOCK)).astype(jnp.int32)
    activations = gaussian(splits[7], (N_DP, SLOTS, ROWS, FF_W), 1.0, 6.0, ((0, 4), (1, 128)))
    return dict(slot_grads=slot_grads, momentum=momentum, master_weights=master_weights, current_slots=current_slots, next_slots=next_slots, live_counts=live_counts, route_index=route_index, activations=activations)


momentum_decay = 0.9
step_rate = 0.5
epsilon = 1e-6
range_limit = 448.0


def reference(slot_grads, momentum, master_weights, current_slots, next_slots, live_counts, route_index, activations):
    owners = current_slots[:, 0].astype(jnp.int32)

    def accumulate(slot_index, totals):
        slot_index = jnp.asarray(slot_index).astype(jnp.int32)
        taken = lax.dynamic_index_in_dim(slot_grads, slot_index, 1, keepdims=False)
        summed = jnp.sum(taken.astype(jnp.float32), axis=0)
        return totals.at[:, owners[slot_index], :].add(summed)

    totals = lax.fori_loop(0, SLOTS, accumulate, jnp.zeros((FF_W, EXPERTS, D), jnp.float32))
    new_momentum = momentum_decay * momentum + totals
    weights = master_weights - step_rate * new_momentum
    blocks = weights.reshape(FF_W, EXPERTS, D // QBLOCK, QBLOCK)
    previous = master_weights.reshape(FF_W, EXPERTS, D // QBLOCK, QBLOCK)
    scales = (jnp.max(jnp.abs(previous), axis=3) / range_limit + epsilon).astype(jnp.bfloat16)
    scaled = blocks / scales.astype(jnp.float32)[:, :, :, None]
    quantized = jnp.clip(scaled, -range_limit, range_limit).astype(jnp.bfloat16)
    restored = (quantized.astype(jnp.float32) * scales.astype(jnp.float32)[:, :, :, None]).astype(jnp.bfloat16)
    restored = restored.reshape(FF_W, EXPERTS, D)
    chosen = next_slots[:, 0].astype(jnp.int32)
    row_numbers = jnp.arange(ROWS, dtype=jnp.int32)

    def per_slot(slot_index):
        weight = lax.dynamic_index_in_dim(restored, chosen[slot_index], 1, keepdims=False)
        inputs = lax.dynamic_index_in_dim(activations, slot_index, 1, keepdims=False)
        indices = lax.dynamic_index_in_dim(route_index, slot_index, 1, keepdims=False)
        counts = lax.dynamic_index_in_dim(live_counts, slot_index, 1, keepdims=False)
        blocked = inputs.reshape(N_DP, ROWS // RBLOCK, RBLOCK, FF_W)
        selected = jnp.take_along_axis(blocked, indices[:, :, :, None], axis=2).reshape(N_DP * ROWS, FF_W)
        product = jnp.dot(selected, weight, preferred_element_type=jnp.float32).reshape(N_DP, ROWS, D)
        live = row_numbers[None, :] < counts[:, None]
        return jnp.where(live[:, :, None], product, 0.0).astype(jnp.bfloat16)

    outputs = lax.map(per_slot, jnp.arange(SLOTS, dtype=jnp.int32))
    expert_out = jnp.transpose(outputs, (1, 0, 2, 3))
    return new_momentum, expert_out
```

```python
import functools

import jax
import jax.numpy as jnp
from jax import lax
from jax.experimental import pallas as pl
from jax.experimental.pallas import tpu as pltpu
from jax.sharding import PartitionSpec as P

MESH = pl.DeviceIdType.MESH
QBLOCK = 128
NY, NX, NZ, NC = 4, 4, 16, 2
NS = NX * NC
CHUNKS = 4

momentum_decay = 0.9
step_rate = 0.5
epsilon = 1e-06
range_limit = 448.0
BF = jnp.bfloat16
F32 = jnp.float32


def idiv(v, d):
    if d == 3:
        return (v * 171) >> 9
    return idiv(v >> (3 if d == 24 else 4), 3)


def split_jip(r):
    j = idiv(r, 24)
    rem = r - j * 24
    i = idiv(rem, 3)
    return j, i, rem - i * 3


def split_ijp(r):
    i = idiv(r, 48)
    rem = r - i * 48
    j = idiv(rem, 3)
    return i, j, rem - j * 3


def dot(a, b):
    return jnp.dot(a, b, preferred_element_type=F32)


def iota(shape, dim):
    return lax.broadcasted_iota(jnp.int32, shape, dim)


def onehot(cond):
    return jnp.where(cond, 1.0, 0.0).astype(BF)


def kernel(
    C,
    grad, mom, mas, cur, nxt, live, route, act,
    nm_out, out,
    gs, mom_v, mas_v, act_v,
    rl, rr, sa1, sa2, pleft, pright,
    zs1, zr1, ss1, sr1, ss2, sr2, zs2, zr2, wl, wr, wo,
    selp, p1, p2, p3, m1, m2,
    lsem, asend, arecv, zsend, zrecv, ssend, srecv, dsend, drecv,
):
    n = CHUNKS
    e = lax.axis_index("expert")
    y = lax.axis_index("dp")
    x, z, c = e // (NZ * NC), (e // NC) % NZ, e % NC
    rows = grad.shape[0]
    half = rows // 2

    def at(dy=0, dx=0, dz=0, dc=0):
        ex = (lax.rem(x + dx, NX) * NZ + lax.rem(z + dz, NZ)) * NC + lax.rem(c + dc, NC)
        return (lax.rem(y + dy, NY), ex)

    def at_i(i):
        return at(dx=i // NC, dc=i % NC)

    def remote(src, dst, ssem, rsem, device):
        return pltpu.make_async_remote_copy(
            src_ref=src, dst_ref=dst, send_sem=ssem, recv_sem=rsem,
            device_id=device, device_id_type=MESH,
        )

    barrier = pltpu.get_barrier_semaphore()
    peers = [at(dz=j) for j in range(1, NZ)]
    peers += [at_i(i) for i in range(1, NS)]
    peers += [at(dy=1), at(dy=3)]
    for device in peers:
        pl.semaphore_signal(barrier, inc=1, device_id=device, device_id_type=MESH)

    locals_ = {}
    k_width = C * n
    for k in range(n):
        for b in (2, 1, 3, 0):
            off = pl.multiple_of(lax.rem(y + b, NY) * k_width + k * C, 128)
            cp = pltpu.make_async_copy(grad.at[:, pl.ds(off, C)], gs.at[b, k], lsem.at[b * n + k])
            cp.start()
            locals_[b, k] = cp
    cp_act = pltpu.make_async_copy(act, act_v, lsem.at[4 * n])
    cp_mom = pltpu.make_async_copy(mom, mom_v, lsem.at[4 * n + 1])
    cp_mas = pltpu.make_async_copy(mas, mas_v, lsem.at[4 * n + 2])
    cp_act.start()
    cp_mom.start()
    cp_mas.start()

    r_col = iota((rows, 1), 0)
    r_row = iota((1, rows), 1)
    lanes = iota((rows, rows), 1)
    subl = iota((rows, rows), 0)
    j, i, p = split_jip(r_col)
    dx, dc = i >> 1, i & 1
    dest = ((x + dx) & 3) * 96 + ((z + j) & 15) * 6 + ((c + dc) & 1) * 3 + p
    p1[...] = onehot(lanes == dest)
    p3[...] = onehot(lanes == i * 48 + j * 3 + p)
    i, j, p = split_ijp(r_col)
    p2[...] = onehot(lanes == j * 24 + i * 3 + p)
    dx, dc = i >> 1, i & 1
    nslot = (((x + dx) & 3) * NZ + ((z + j) & 15)) * NC + ((c + dc) & 1)
    pick = onehot(iota((rows, 128), 1) == nslot)
    experts = mom_v.shape[1]
    three = 3 * experts
    nvals = jnp.broadcast_to(nxt[...].astype(F32), (128, three)).astype(BF)
    expert_of = dot(pick, nvals).astype(jnp.int32)
    m2[...] = onehot(expert_of + experts * p == iota((rows, three), 1))

    i, j, p = split_ijp(r_row)
    dx, dc = i >> 1, i & 1
    cslot = (((x - dx) & 3) * NZ + ((z - j) & 15)) * NC + ((c + dc) & 1)
    pick = onehot(iota((128, rows), 0) == cslot)
    cvals = jnp.broadcast_to(cur[...].astype(F32), (128, 128)).T.astype(BF)
    expert_of = dot(cvals, pick).astype(jnp.int32)[0:1, :]
    m1[...] = onehot(expert_of + experts * p == iota((three, rows), 0))

    j, i, p = split_jip(r_row)
    dx, dc = i >> 1, i & 1
    source = ((x - dx) & 3) * 96 + ((z - j) & 15) * 6 + ((c + dc) & 1) * 3 + p
    p4 = onehot(subl == source)
    cp_act.wait()
    blocks, rb = route.shape
    for q in range(blocks):
        hit = jnp.where(route[q : q + 1, :] == iota((rb, rb), 0), 1.0, 0.0).astype(F32)
        picked = dot(hit.T.astype(BF), act_v[q * rb : (q + 1) * rb, :])
        alive = iota((rb, 1), 0) + q * rb < live[...]
        picked = jnp.where(alive, picked, 0.0).astype(BF)
        selp[q * rb : (q + 1) * rb, :] = dot(picked, p4).astype(BF)

    pl.semaphore_wait(barrier, len(peers))

    ends = []

    def a1(k):
        for b in (2, 1, 3):
            locals_[b, k].wait()
        up, down = at(dy=1), at(dy=3)
        lo, hi = pl.ds(0, half), pl.ds(half, half)
        for args in (
            (gs.at[2, k, lo], rl.at[k], asend.at[0, k], arecv.at[0, k], up),
            (gs.at[2, k, hi], rr.at[k], asend.at[1, k], arecv.at[1, k], down),
            (gs.at[1, k, hi], pleft.at[k, hi], asend.at[2, k], arecv.at[2, k], up),
            (gs.at[3, k, lo], pright.at[k, lo], asend.at[3, k], arecv.at[3, k], down),
        ):
            cp = remote(*args)
            cp.start()
            ends.append(cp)

    def a2(k):
        up, down = at(dy=1), at(dy=3)
        lo, hi = pl.ds(0, half), pl.ds(half, half)
        remote(rl.at[k], rl.at[k], asend.at[0, k], arecv.at[0, k], up).wait_recv()
        sa1[k] = (gs[1, k, 0:half].astype(F32) + rl[k].astype(F32)).astype(BF)
        cp = remote(sa1.at[k], pleft.at[k, lo], asend.at[4, k], arecv.at[2, k], up)
        cp.start()
        ends.append(cp)
        remote(rr.at[k], rr.at[k], asend.at[1, k], arecv.at[1, k], down).wait_recv()
        sa2[k] = (gs[3, k, half:].astype(F32) + rr[k].astype(F32)).astype(BF)
        cp = remote(sa2.at[k], pright.at[k, hi], asend.at[5, k], arecv.at[3, k], down)
        cp.start()
        ends.append(cp)

    def exchange_z(k, send, recv, s):
        for j in range(1, NZ):
            remote(send.at[k, j], recv.at[k, j], zsend.at[s, k], zrecv.at[s, k], at(dz=j)).start()
        every = pl.ds(1, NZ - 1)
        ends.append(remote(send.at[k, every], recv.at[k, every], zsend.at[s, k], zrecv.at[s, k], at(dz=1)))

    def arrived_z(k, recv, s):
        every = pl.ds(1, NZ - 1)
        remote(recv.at[k, every], recv.at[k, every], zsend.at[s, k], zrecv.at[s, k], at(dz=1)).wait_recv()

    def exchange_s(k, send, recv, s):
        for i in range(NS - 1, 0, -1):
            remote(send.at[k, i], recv.at[k, i], ssend.at[s, k], srecv.at[s, k], at_i(i)).start()
        every = pl.ds(1, NS - 1)
        ends.append(remote(send.at[k, every], recv.at[k, every], ssend.at[s, k], srecv.at[s, k], at_i(1)))

    def arrived_s(k, recv, s):
        every = pl.ds(1, NS - 1)
        remote(recv.at[k, every], recv.at[k, every], ssend.at[s, k], srecv.at[s, k], at_i(1)).wait_recv()

    def a3(k):
        remote(pleft.at[k], pleft.at[k], asend.at[2, k], arecv.at[2, k], at(dy=1)).wait_recv()
        remote(pright.at[k], pright.at[k], asend.at[3, k], arecv.at[3, k], at(dy=3)).wait_recv()
        locals_[0, k].wait()
        total = gs[0, k].astype(F32) + pleft[k].astype(F32) + pright[k].astype(F32)
        moved = dot(p1[...], total.astype(BF)).reshape(NZ, 24, C).astype(BF)
        zs1[k] = moved
        zr1[k, 0] = moved[0]
        exchange_z(k, zs1, zr1, 0)

    def b1(k):
        arrived_z(k, zr1, 0)
        held = zr1[k].astype(F32).reshape(rows, C).astype(BF)
        moved = dot(p2[...], held).reshape(NS, 48, C).astype(BF)
        ss1[k] = moved
        sr1[k, 0] = moved[0]
        exchange_s(k, ss1, sr1, 0)

    def b2(k):
        arrived_s(k, sr1, 0)
        totals = dot(m1[...], sr1[k].reshape(rows, C))
        cols = slice(k * C, (k + 1) * C)
        new_momentum = momentum_decay * mom_v[:, :, cols].reshape(three, C) + totals
        nm_out[:, :, cols] = new_momentum.reshape(3, experts, C)
        master = mas_v[:, :, cols].reshape(three, C)
        weights = master - step_rate * new_momentum
        parts = []
        for b in range(C // QBLOCK):
            lanes_b = slice(b * QBLOCK, (b + 1) * QBLOCK)
            top = jnp.max(jnp.abs(master[:, lanes_b]), axis=1, keepdims=True)
            scale = (top / range_limit + epsilon).astype(BF).astype(F32)
            quantized = jnp.clip(weights[:, lanes_b] / scale, -range_limit, range_limit).astype(BF)
            parts.append((quantized.astype(F32) * scale).astype(BF))
        restored = parts[0] if len(parts) == 1 else jnp.concatenate(parts, axis=1)
        moved = dot(m2[...], restored).reshape(NS, 48, C).astype(BF)
        ss2[k] = moved
        sr2[k, 0] = moved[0]
        exchange_s(k, ss2, sr2, 1)

    def c1(k):
        arrived_s(k, sr2, 1)
        moved = dot(p3[...], sr2[k].reshape(rows, C)).reshape(NZ, 24, C).astype(BF)
        zs2[k] = moved
        zr2[k, 0] = moved[0]
        exchange_z(k, zs2, zr2, 1)

    lo8, hi8 = pl.ds(0, NZ // 2), pl.ds(NZ // 2, NZ // 2)

    def d1(k):
        arrived_z(k, zr2, 1)
        up, down = at(dy=1), at(dy=3)
        for args in (
            (zr2.at[k, lo8], wl.at[k, lo8], dsend.at[0, k], drecv.at[0, k], up),
            (zr2.at[k, hi8], wr.at[k, hi8], dsend.at[1, k], drecv.at[1, k], down),
            (zr2.at[k, hi8], wl.at[k, hi8], dsend.at[2, k], drecv.at[2, k], up),
            (zr2.at[k, lo8], wr.at[k, lo8], dsend.at[3, k], drecv.at[3, k], down),
        ):
            cp = remote(*args)
            cp.start()
            ends.append(cp)

    def multiply(k, held, b):
        weight = held[k].astype(F32).reshape(rows, C).astype(BF)
        product = dot(selp[...], weight).astype(BF)
        off = pl.multiple_of(lax.rem(y + b, NY) * k_width + k * C, 128)
        out[:, pl.ds(off, C)] = product

    def d2(k):
        up, down = at(dy=1), at(dy=3)
        remote(wl.at[k, lo8], wl.at[k, lo8], dsend.at[0, k], drecv.at[0, k], up).wait_recv()
        cp = remote(wl.at[k, lo8], wo.at[k, lo8], dsend.at[4, k], drecv.at[4, k], up)
        cp.start()
        ends.append(cp)
        remote(wr.at[k, hi8], wr.at[k, hi8], dsend.at[1, k], drecv.at[1, k], down).wait_recv()
        cp = remote(wr.at[k, hi8], wo.at[k, hi8], dsend.at[5, k], drecv.at[5, k], down)
        cp.start()
        ends.append(cp)
        multiply(k, zr2, 0)

    def d3(k):
        up, down = at(dy=1), at(dy=3)
        remote(wl.at[k, hi8], wl.at[k, hi8], dsend.at[2, k], drecv.at[2, k], up).wait_recv()
        multiply(k, wl, 3)
        remote(wr.at[k, lo8], wr.at[k, lo8], dsend.at[3, k], drecv.at[3, k], down).wait_recv()
        multiply(k, wr, 1)
        remote(wo.at[k, lo8], wo.at[k, lo8], dsend.at[4, k], drecv.at[4, k], up).wait_recv()
        remote(wo.at[k, hi8], wo.at[k, hi8], dsend.at[5, k], drecv.at[5, k], down).wait_recv()
        multiply(k, wo, 2)

    a1(0); a1(1); a2(0); a3(0); a1(2)
    cp_mom.wait()
    cp_mas.wait()
    a2(1); a3(1); a1(3); a2(2); a3(2); b1(0)
    a2(3); a3(3); b2(0); b1(1); c1(0); b2(1); b1(2); c1(1); b2(2); b1(3); c1(2); b2(3)
    d1(0); c1(3); d2(0); d1(1); d3(0); d2(1); d1(2); d3(1); d2(2); d1(3); d3(2); d2(3); d3(3)
    for cp in ends:
        cp.wait_send()


def shards(grads, momentum, master, current_slots, next_slots, live_counts, route_index, activations):
    grad = grads[0, 0]
    rows, width = grad.shape
    columns = momentum.shape[2]
    experts = momentum.shape[1]
    n = CHUNKS
    C = columns // n
    out_rows, hidden = activations.shape[2:]
    half = rows // 2
    any_ = pl.BlockSpec(memory_space=pl.ANY)
    vmem = pl.BlockSpec(memory_space=pltpu.VMEM)

    def buf(*shape):
        return pltpu.VMEM(shape, BF)

    zbuf = buf(n, NZ, 24, C)
    sbuf = buf(n, NS, 48, C)
    sems = pltpu.SemaphoreType.DMA
    new_momentum, expert_out = pl.pallas_call(
        functools.partial(kernel, C),
        out_shape=(
            jax.ShapeDtypeStruct(momentum.shape, F32),
            jax.ShapeDtypeStruct((out_rows, width), BF),
        ),
        in_specs=[any_, any_, any_, vmem, vmem, vmem, vmem, any_],
        out_specs=(vmem, vmem),
        scratch_shapes=[
            buf(NY, n, rows, C),
            pltpu.VMEM(momentum.shape, F32),
            pltpu.VMEM(momentum.shape, F32),
            buf(out_rows, hidden),
            buf(n, half, C), buf(n, half, C), buf(n, half, C), buf(n, half, C),
            buf(n, rows, C), buf(n, rows, C),
            zbuf, zbuf, sbuf, sbuf, sbuf, sbuf, zbuf, zbuf, zbuf, zbuf, zbuf,
            buf(out_rows, hidden),
            buf(rows, rows), buf(rows, rows), buf(rows, rows),
            buf(3 * experts, rows), buf(rows, 3 * experts),
            sems((4 * n + 3,)),
            sems((6, n)), sems((4, n)),
            sems((2, n)), sems((2, n)),
            sems((2, n)), sems((2, n)),
            sems((6, n)), sems((6, n)),
        ],
        compiler_params=pltpu.CompilerParams(
            collective_id=0, has_side_effects=True, vmem_limit_bytes=40 * 1024 * 1024
        ),
        name="step",
    )(
        grad, momentum, master, current_slots, next_slots, live_counts,
        route_index[0, 0], activations[0, 0],
    )
    return new_momentum, expert_out[None, None]


def solution(mesh):
    in_specs = (
        P("dp", "expert", None, None),
        P("expert", None, "dp"),
        P("expert", None, "dp"),
        P(),
        P(),
        P("dp", "expert"),
        P("dp", "expert", None, None),
        P("dp", "expert", None, None),
    )
    out_specs = (P("expert", None, "dp"), P("dp", "expert", None, None))
    return jax.shard_map(shards, mesh=mesh, in_specs=in_specs, out_specs=out_specs, check_vma=False)
```

```python
import functools

import jax
import jax.numpy as jnp
from jax import lax
from jax.experimental import pallas as pl
from jax.experimental.pallas import tpu as pltpu
from jax.sharding import PartitionSpec as P

MESH = pl.DeviceIdType.MESH
QBLOCK = 128
NY, NX, NZ, NC = 4, 4, 16, 2
NS = NX * NC
CHUNKS = 4

momentum_decay = 0.9
step_rate = 0.5
epsilon = 1e-06
range_limit = 448.0
BF = jnp.bfloat16
F32 = jnp.float32


def idiv(v, d):
    if d == 3:
        return (v * 171) >> 9
    return idiv(v >> (3 if d == 24 else 4), 3)


def split_jip(r):
    j = idiv(r, 24)
    rem = r - j * 24
    i = idiv(rem, 3)
    return j, i, rem - i * 3


def split_ijp(r):
    i = idiv(r, 48)
    rem = r - i * 48
    j = idiv(rem, 3)
    return i, j, rem - j * 3


def dot(a, b):
    return jnp.dot(a, b, preferred_element_type=F32)


def iota(shape, dim):
    return lax.broadcasted_iota(jnp.int32, shape, dim)


def onehot(cond):
    return jnp.where(cond, 1.0, 0.0).astype(BF)


def kernel(
    C,
    grad, mom, mas, cur_h, nxt_h, live, route_h, act,
    nm_out, out,
    gs, mom_v, mas_v, act_v, cur, nxt, route,
    rl, rr, sa1, sa2, pleft, pright,
    zs1, zr1, ss1, sr1, ss2, sr2, zs2, zr2, wl, wr, wo,
    selp, p1, p2, p3, p4, m1, m2,
    lsem, asend, arecv, zsend, zrecv, ssend, srecv, dsend, drecv, tsem,
):
    n = CHUNKS
    e = lax.axis_index("expert")
    y = lax.axis_index("dp")
    x, z, c = e // (NZ * NC), (e // NC) % NZ, e % NC
    rows = grad.shape[0]
    half = rows // 2

    def at(dy=0, dx=0, dz=0, dc=0):
        ex = (lax.rem(x + dx, NX) * NZ + lax.rem(z + dz, NZ)) * NC + lax.rem(c + dc, NC)
        return (lax.rem(y + dy, NY), ex)

    def at_i(i):
        return at(dx=i // NC, dc=i % NC)

    def remote(src, dst, ssem, rsem, device):
        return pltpu.make_async_remote_copy(
            src_ref=src, dst_ref=dst, send_sem=ssem, recv_sem=rsem,
            device_id=device, device_id_type=MESH,
        )

    barrier = pltpu.get_barrier_semaphore()
    peers = [at(dz=1), at(dz=NZ - 1)]
    peers += [at_i(i) for i in range(1, NS)]
    peers += [at(dy=1), at(dy=3)]
    for device in peers:
        pl.semaphore_signal(barrier, inc=1, device_id=device, device_id_type=MESH)

    staged = {}
    k_width = C * n
    for k in range(n):
        for b in (2, 1, 3, 0):
            off = pl.multiple_of(lax.rem(y + b, NY) * k_width + k * C, 128)
            staged[b, k] = pltpu.make_async_copy(grad.at[:, pl.ds(off, C)], gs.at[b, k], lsem.at[b * n + k])
    small = [(act, act_v), (route_h, route), (cur_h, cur), (nxt_h, nxt), (mom, mom_v), (mas, mas_v)]
    small = [pltpu.make_async_copy(src, dst, lsem.at[4 * n + at_]) for at_, (src, dst) in enumerate(small)]
    cp_act, cp_route, cp_cur, cp_nxt, cp_mom, cp_mas = small
    for k in range(n):
        for b in (2, 1, 3, 0):
            staged[b, k].start()
    for cp in (cp_cur, cp_nxt, cp_route, cp_act, cp_mom, cp_mas):
        cp.start()

    experts = mom_v.shape[1]
    three = 3 * experts

    def build_p1():
        j, i, p = split_jip(iota((rows, 1), 0))
        dest = ((x + (i >> 1)) & 3) * 96 + ((z + j) & 15) * 6 + ((c + (i & 1)) & 1) * 3 + p
        p1[...] = onehot(iota((rows, rows), 1) == dest)

    def build_p2():
        i, j, p = split_ijp(iota((rows, 1), 0))
        p2[...] = onehot(iota((rows, rows), 1) == j * 24 + i * 3 + p)

    def build_p3():
        j, i, p = split_jip(iota((rows, 1), 0))
        p3[...] = onehot(iota((rows, rows), 1) == i * 48 + j * 3 + p)

    def build_m1():
        i, j, p = split_ijp(iota((1, rows), 1))
        slot = (((x - (i >> 1)) & 3) * NZ + ((z - j) & 15)) * NC + ((c + (i & 1)) & 1)
        pick = onehot(iota((128, rows), 0) == slot)
        cp_cur.wait()
        values = jnp.broadcast_to(cur[...].astype(F32), (16, 128)).astype(BF)
        expert_of = dot(values, pick).astype(jnp.int32)[0:1, :]
        m1[...] = onehot(expert_of + experts * p == iota((three, rows), 0))

    def build_m2():
        i, j, p = split_ijp(iota((rows, 1), 0))
        slot = (((x + (i >> 1)) & 3) * NZ + ((z + j) & 15)) * NC + ((c + (i & 1)) & 1)
        pick = onehot(iota((rows, 128), 1) == slot)
        cp_nxt.wait()
        values = jnp.broadcast_to(nxt[...].astype(F32), (128, 128)).T.astype(BF)
        values = jnp.concatenate([values, values], axis=1)[:, 0:three]
        expert_of = dot(pick, values).astype(jnp.int32)
        m2[...] = onehot(expert_of + experts * p == iota((rows, three), 1))

    def build_p4():
        j, i, p = split_jip(iota((1, rows), 1))
        source = ((x - (i >> 1)) & 3) * 96 + ((z - j) & 15) * 6 + ((c + (i & 1)) & 1) * 3 + p
        p4[...] = onehot(iota((rows, rows), 0) == source)
        cp_act.wait()
        cp_route.wait()

    def select(q):
        rb = route.shape[1]
        hit = jnp.where(route[q : q + 1, :] == iota((rb, rb), 0), 1.0, 0.0).astype(F32)
        picked = dot(hit.T.astype(BF), act_v[q * rb : (q + 1) * rb, :])
        alive = iota((rb, 1), 0) + q * rb < live[...]
        picked = jnp.where(alive, picked, 0.0).astype(BF)
        selp[q * rb : (q + 1) * rb, :] = dot(picked, p4[...]).astype(BF)

    pl.semaphore_wait(barrier, len(peers))

    ends = []

    def tell(r):
        for way, dz in ((0, 1 << r), (1, NZ - (1 << r))):
            pl.semaphore_signal(tsem.at[r, way], inc=1, device_id=at(dz=dz), device_id_type=MESH)

    def hear(r):
        pl.semaphore_wait(tsem.at[r, 0], 1)
        pl.semaphore_wait(tsem.at[r, 1], 1)

    def a1(k):
        for b in (2, 1, 3):
            staged[b, k].wait()
        up, down = at(dy=1), at(dy=3)
        lo, hi = pl.ds(0, half), pl.ds(half, half)
        for args in (
            (gs.at[2, k, lo], rl.at[k], asend.at[0, k], arecv.at[0, k], up),
            (gs.at[2, k, hi], rr.at[k], asend.at[1, k], arecv.at[1, k], down),
            (gs.at[1, k, hi], pleft.at[k, hi], asend.at[2, k], arecv.at[2, k], up),
            (gs.at[3, k, lo], pright.at[k, lo], asend.at[3, k], arecv.at[3, k], down),
        ):
            cp = remote(*args)
            cp.start()
            ends.append(cp)

    def a2(k):
        up, down = at(dy=1), at(dy=3)
        lo, hi = pl.ds(0, half), pl.ds(half, half)
        remote(rl.at[k], rl.at[k], asend.at[0, k], arecv.at[0, k], up).wait_recv()
        sa1[k] = (gs[1, k, 0:half].astype(F32) + rl[k].astype(F32)).astype(BF)
        cp = remote(sa1.at[k], pleft.at[k, lo], asend.at[4, k], arecv.at[2, k], up)
        cp.start()
        ends.append(cp)
        remote(rr.at[k], rr.at[k], asend.at[1, k], arecv.at[1, k], down).wait_recv()
        sa2[k] = (gs[3, k, half:].astype(F32) + rr[k].astype(F32)).astype(BF)
        cp = remote(sa2.at[k], pright.at[k, hi], asend.at[5, k], arecv.at[3, k], down)
        cp.start()
        ends.append(cp)

    def exchange_z(k, send, recv, s):
        for j in range(1, NZ):
            remote(send.at[k, j], recv.at[k, j], zsend.at[s, k], zrecv.at[s, k], at(dz=j)).start()
        every = pl.ds(1, NZ - 1)
        ends.append(remote(send.at[k, every], recv.at[k, every], zsend.at[s, k], zrecv.at[s, k], at(dz=1)))

    def arrived_z(k, recv, s):
        every = pl.ds(1, NZ - 1)
        remote(recv.at[k, every], recv.at[k, every], zsend.at[s, k], zrecv.at[s, k], at(dz=1)).wait_recv()

    def exchange_s(k, send, recv, s):
        for i in range(NS - 1, 0, -1):
            remote(send.at[k, i], recv.at[k, i], ssend.at[s, k], srecv.at[s, k], at_i(i)).start()
        every = pl.ds(1, NS - 1)
        ends.append(remote(send.at[k, every], recv.at[k, every], ssend.at[s, k], srecv.at[s, k], at_i(1)))

    def arrived_s(k, recv, s):
        every = pl.ds(1, NS - 1)
        remote(recv.at[k, every], recv.at[k, every], ssend.at[s, k], srecv.at[s, k], at_i(1)).wait_recv()

    def a3(k):
        remote(pleft.at[k], pleft.at[k], asend.at[2, k], arecv.at[2, k], at(dy=1)).wait_recv()
        remote(pright.at[k], pright.at[k], asend.at[3, k], arecv.at[3, k], at(dy=3)).wait_recv()
        staged[0, k].wait()
        total = gs[0, k].astype(F32) + pleft[k].astype(F32) + pright[k].astype(F32)
        moved = dot(p1[...], total.astype(BF)).reshape(NZ, 24, C).astype(BF)
        zs1[k] = moved
        zr1[k, 0] = moved[0]
        exchange_z(k, zs1, zr1, 0)

    def b1(k):
        arrived_z(k, zr1, 0)
        held = zr1[k].astype(F32).reshape(rows, C).astype(BF)
        moved = dot(p2[...], held).reshape(NS, 48, C).astype(BF)
        ss1[k] = moved
        sr1[k, 0] = moved[0]
        exchange_s(k, ss1, sr1, 0)

    def b2(k):
        arrived_s(k, sr1, 0)
        totals = dot(m1[...], sr1[k].reshape(rows, C))
        cols = slice(k * C, (k + 1) * C)
        new_momentum = momentum_decay * mom_v[:, :, cols].reshape(three, C) + totals
        nm_out[:, :, cols] = new_momentum.reshape(3, experts, C)
        master = mas_v[:, :, cols].reshape(three, C)
        weights = master - step_rate * new_momentum
        parts = []
        for b in range(C // QBLOCK):
            lanes_b = slice(b * QBLOCK, (b + 1) * QBLOCK)
            top = jnp.max(jnp.abs(master[:, lanes_b]), axis=1, keepdims=True)
            scale = (top / range_limit + epsilon).astype(BF).astype(F32)
            quantized = jnp.clip(weights[:, lanes_b] / scale, -range_limit, range_limit).astype(BF)
            parts.append((quantized.astype(F32) * scale).astype(BF))
        restored = parts[0] if len(parts) == 1 else jnp.concatenate(parts, axis=1)
        moved = dot(m2[...], restored).reshape(NS, 48, C).astype(BF)
        ss2[k] = moved
        sr2[k, 0] = moved[0]
        exchange_s(k, ss2, sr2, 1)

    def c1(k):
        arrived_s(k, sr2, 1)
        moved = dot(p3[...], sr2[k].reshape(rows, C)).reshape(NZ, 24, C).astype(BF)
        zs2[k] = moved
        zr2[k, 0] = moved[0]
        exchange_z(k, zs2, zr2, 1)

    lo8, hi8 = pl.ds(0, NZ // 2), pl.ds(NZ // 2, NZ // 2)

    def d1(k):
        arrived_z(k, zr2, 1)
        up, down = at(dy=1), at(dy=3)
        for args in (
            (zr2.at[k, lo8], wl.at[k, lo8], dsend.at[0, k], drecv.at[0, k], up),
            (zr2.at[k, hi8], wr.at[k, hi8], dsend.at[1, k], drecv.at[1, k], down),
            (zr2.at[k, hi8], wl.at[k, hi8], dsend.at[2, k], drecv.at[2, k], up),
            (zr2.at[k, lo8], wr.at[k, lo8], dsend.at[3, k], drecv.at[3, k], down),
        ):
            cp = remote(*args)
            cp.start()
            ends.append(cp)

    def multiply(k, held, b):
        weight = held[k].astype(F32).reshape(rows, C).astype(BF)
        product = dot(selp[...], weight).astype(BF)
        off = pl.multiple_of(lax.rem(y + b, NY) * k_width + k * C, 128)
        out[:, pl.ds(off, C)] = product

    def d2(k):
        up, down = at(dy=1), at(dy=3)
        remote(wl.at[k, lo8], wl.at[k, lo8], dsend.at[0, k], drecv.at[0, k], up).wait_recv()
        cp = remote(wl.at[k, lo8], wo.at[k, lo8], dsend.at[4, k], drecv.at[4, k], up)
        cp.start()
        ends.append(cp)
        remote(wr.at[k, hi8], wr.at[k, hi8], dsend.at[1, k], drecv.at[1, k], down).wait_recv()
        cp = remote(wr.at[k, hi8], wo.at[k, hi8], dsend.at[5, k], drecv.at[5, k], down)
        cp.start()
        ends.append(cp)
        multiply(k, zr2, 0)

    def d3(k):
        up, down = at(dy=1), at(dy=3)
        remote(wl.at[k, hi8], wl.at[k, hi8], dsend.at[2, k], drecv.at[2, k], up).wait_recv()
        multiply(k, wl, 3)
        remote(wr.at[k, lo8], wr.at[k, lo8], dsend.at[3, k], drecv.at[3, k], down).wait_recv()
        multiply(k, wr, 1)
        remote(wo.at[k, lo8], wo.at[k, lo8], dsend.at[4, k], drecv.at[4, k], up).wait_recv()
        remote(wo.at[k, hi8], wo.at[k, hi8], dsend.at[5, k], drecv.at[5, k], down).wait_recv()
        multiply(k, wo, 2)

    a1(0); tell(0); a1(1); build_p1(); hear(0); tell(1); a2(0); hear(1); tell(2); a1(2); build_p2(); hear(2); a3(0)
    a2(1); build_m1(); build_m2(); a3(1); a1(3); a2(2); build_p3(); build_p4(); a3(2)
    cp_mom.wait()
    cp_mas.wait()
    b1(0); select(0); a2(3); a3(3); b2(0); b1(1); select(1); c1(0); b2(1); b1(2); c1(1); b2(2); b1(3)
    c1(2); b2(3); select(2); select(3); d1(0); c1(3); d2(0); d1(1); d3(0); d2(1); d1(2); d3(1); d2(2); d1(3); d3(2); d2(3); d3(3)
    for cp in ends:
        cp.wait_send()


def shards(grads, momentum, master, current_slots, next_slots, live_counts, route_index, activations):
    grad = grads[0, 0]
    rows, width = grad.shape
    columns = momentum.shape[2]
    experts = momentum.shape[1]
    n = CHUNKS
    C = columns // n
    out_rows, hidden = activations.shape[2:]
    half = rows // 2
    hbm = pl.BlockSpec(memory_space=pltpu.MemorySpace.HBM)
    vmem = pl.BlockSpec(memory_space=pltpu.VMEM)

    def buf(*shape):
        return pltpu.VMEM(shape, BF)

    zbuf = buf(n, NZ, 24, C)
    sbuf = buf(n, NS, 48, C)
    sems = pltpu.SemaphoreType.DMA
    held = lambda a: pltpu.with_memory_space_constraint(a, pltpu.MemorySpace.HBM)
    new_momentum, expert_out = pl.pallas_call(
        functools.partial(kernel, C),
        out_shape=(
            jax.ShapeDtypeStruct(momentum.shape, F32),
            jax.ShapeDtypeStruct((out_rows, width), BF),
        ),
        in_specs=[hbm, hbm, hbm, hbm, hbm, vmem, hbm, hbm],
        out_specs=(vmem, vmem),
        scratch_shapes=[
            buf(NY, n, rows, C),
            pltpu.VMEM(momentum.shape, F32),
            pltpu.VMEM(momentum.shape, F32),
            buf(out_rows, hidden),
            pltpu.VMEM((1, current_slots.shape[0]), jnp.int32),
            pltpu.VMEM((1, current_slots.shape[0]), jnp.int32),
            pltpu.VMEM(route_index.shape[2:], jnp.int32),
            buf(n, half, C), buf(n, half, C), buf(n, half, C), buf(n, half, C),
            buf(n, rows, C), buf(n, rows, C),
            zbuf, zbuf, sbuf, sbuf, sbuf, sbuf, zbuf, zbuf, zbuf, zbuf, zbuf,
            buf(out_rows, hidden),
            buf(rows, rows), buf(rows, rows), buf(rows, rows), buf(rows, rows),
            buf(3 * experts, rows), buf(rows, 3 * experts),
            sems((4 * n + 6,)),
            sems((6, n)), sems((4, n)),
            sems((2, n)), sems((2, n)),
            sems((2, n)), sems((2, n)),
            sems((6, n)), sems((6, n)),
            pltpu.SemaphoreType.REGULAR((3, 2)),
        ],
        compiler_params=pltpu.CompilerParams(
            collective_id=0, has_side_effects=True, vmem_limit_bytes=40 * 1024 * 1024
        ),
        name="step",
    )(
        held(grad), held(momentum), held(master), held(current_slots.reshape(1, -1)), held(next_slots.reshape(1, -1)), live_counts,
        held(route_index[0, 0]), held(activations[0, 0]),
    )
    return new_momentum, expert_out[None, None]


def solution(mesh):
    in_specs = (
        P("dp", "expert", None, None),
        P("expert", None, "dp"),
        P("expert", None, "dp"),
        P(),
        P(),
        P("dp", "expert"),
        P("dp", "expert", None, None),
        P("dp", "expert", None, None),
    )
    out_specs = (P("expert", None, "dp"), P("dp", "expert", None, None))
    return jax.shard_map(shards, mesh=mesh, in_specs=in_specs, out_specs=out_specs, check_vma=False)
```

```python
import functools

import jax
import jax.numpy as jnp
from jax import lax
from jax.experimental import pallas as pl
from jax.experimental.pallas import tpu as pltpu
from jax.sharding import PartitionSpec as P

MESH = pl.DeviceIdType.MESH
QBLOCK = 128
NY, NX, NZ, NC = 4, 4, 16, 2
NS = NX * NC
CHUNKS = 4
FAR_FIRST = sorted(range(1, NZ), key=lambda j: -min(j, NZ - j))

momentum_decay = 0.9
step_rate = 0.5
epsilon = 1e-06
range_limit = 448.0
BF = jnp.bfloat16
F32 = jnp.float32


def idiv(v, d):
    if d == 3:
        return (v * 171) >> 9
    return idiv(v >> (3 if d == 24 else 4), 3)


def split_jip(r):
    j = idiv(r, 24)
    rem = r - j * 24
    i = idiv(rem, 3)
    return j, i, rem - i * 3


def split_ijp(r):
    i = idiv(r, 48)
    rem = r - i * 48
    j = idiv(rem, 3)
    return i, j, rem - j * 3


def dot(a, b):
    return jnp.dot(a, b, preferred_element_type=F32)


def iota(shape, dim):
    return lax.broadcasted_iota(jnp.int32, shape, dim)


def onehot(cond):
    return jnp.where(cond, 1.0, 0.0).astype(BF)


def kernel(
    C,
    grad, mom, mas, cur_h, nxt_h, live, route_h, act,
    nm_out, out,
    gs, mom_v, mas_v, act_v, cur, nxt, route,
    rel, sums, parts_in, zsb, zrb, ssb, srb, wb,
    selp, p1, p2, p3, p4, m1, m2,
    lsem, asend, arecv, zsend, zrecv, ssend, srecv, dsend, drecv, tsem,
):
    n = CHUNKS
    e = lax.axis_index("expert")
    y = lax.axis_index("dp")
    x, z, c = e // (NZ * NC), (e // NC) % NZ, e % NC
    rows = grad.shape[0]
    half = rows // 2

    def at(dy=0, dx=0, dz=0, dc=0):
        ex = (lax.rem(x + dx, NX) * NZ + lax.rem(z + dz, NZ)) * NC + lax.rem(c + dc, NC)
        return (lax.rem(y + dy, NY), ex)

    def at_i(i):
        return at(dx=i // NC, dc=i % NC)

    def remote(src, dst, ssem, rsem, device):
        return pltpu.make_async_remote_copy(
            src_ref=src, dst_ref=dst, send_sem=ssem, recv_sem=rsem,
            device_id=device, device_id_type=MESH,
        )

    barrier = pltpu.get_barrier_semaphore()
    peers = [at(dz=1), at(dz=NZ - 1)]
    peers += [at_i(i) for i in range(1, NS)]
    peers += [at(dy=1), at(dy=3)]
    for device in peers:
        pl.semaphore_signal(barrier, inc=1, device_id=device, device_id_type=MESH)

    k_width = C * n
    for k in range(n):
        for b in (2, 1, 3):
            off = pl.multiple_of(lax.rem(y + b, NY) * k_width + k * C, 128)
            pltpu.make_async_copy(grad.at[:, pl.ds(off, C)], gs.at[b, k], lsem.at[k]).start()
    for k in range(n):
        off = pl.multiple_of(y * k_width + k * C, 128)
        pltpu.make_async_copy(grad.at[:, pl.ds(off, C)], gs.at[0, k], lsem.at[n]).start()
    small = [(act, act_v), (route_h, route), (cur_h, cur), (nxt_h, nxt), (mom, mom_v), (mas, mas_v)]
    small = [pltpu.make_async_copy(src, dst, lsem.at[n + 1 + at_]) for at_, (src, dst) in enumerate(small)]
    cp_act, cp_route, cp_cur, cp_nxt, cp_mom, cp_mas = small
    for cp in (cp_cur, cp_nxt, cp_route, cp_act, cp_mom, cp_mas):
        cp.start()

    def all_of(ref, sem):
        return pltpu.make_async_copy(ref, ref, sem)

    experts = mom_v.shape[1]
    three = 3 * experts

    def build_p1():
        j, i, p = split_jip(iota((rows, 1), 0))
        dest = ((x + (i >> 1)) & 3) * 96 + ((z + j) & 15) * 6 + ((c + (i & 1)) & 1) * 3 + p
        p1[...] = onehot(iota((rows, rows), 1) == dest)

    def build_p2():
        i, j, p = split_ijp(iota((rows, 1), 0))
        p2[...] = onehot(iota((rows, rows), 1) == j * 24 + i * 3 + p)

    def build_p3():
        j, i, p = split_jip(iota((rows, 1), 0))
        p3[...] = onehot(iota((rows, rows), 1) == i * 48 + j * 3 + p)

    def build_m1():
        i, j, p = split_ijp(iota((1, rows), 1))
        slot = (((x - (i >> 1)) & 3) * NZ + ((z - j) & 15)) * NC + ((c + (i & 1)) & 1)
        pick = onehot(iota((128, rows), 0) == slot)
        cp_cur.wait()
        values = jnp.broadcast_to(cur[...].astype(F32), (16, 128)).astype(BF)
        expert_of = dot(values, pick).astype(jnp.int32)[0:1, :]
        m1[...] = onehot(expert_of + experts * p == iota((three, rows), 0))

    def build_m2():
        i, j, p = split_ijp(iota((rows, 1), 0))
        slot = (((x + (i >> 1)) & 3) * NZ + ((z + j) & 15)) * NC + ((c + (i & 1)) & 1)
        pick = onehot(iota((rows, 128), 1) == slot)
        cp_nxt.wait()
        values = jnp.broadcast_to(nxt[...].astype(F32), (128, 128)).T.astype(BF)
        values = jnp.concatenate([values, values], axis=1)[:, 0:three]
        expert_of = dot(pick, values).astype(jnp.int32)
        m2[...] = onehot(expert_of + experts * p == iota((rows, three), 1))

    def build_p4():
        j, i, p = split_jip(iota((1, rows), 1))
        source = ((x - (i >> 1)) & 3) * 96 + ((z - j) & 15) * 6 + ((c + (i & 1)) & 1) * 3 + p
        p4[...] = onehot(iota((rows, rows), 0) == source)
        cp_act.wait()
        cp_route.wait()

    def select(q):
        rb = route.shape[1]
        hit = jnp.where(route[q : q + 1, :] == iota((rb, rb), 0), 1.0, 0.0).astype(F32)
        picked = dot(hit.T.astype(BF), act_v[q * rb : (q + 1) * rb, :])
        alive = iota((rb, 1), 0) + q * rb < live[...]
        picked = jnp.where(alive, picked, 0.0).astype(BF)
        selp[q * rb : (q + 1) * rb, :] = dot(picked, p4[...]).astype(BF)

    pl.semaphore_wait(barrier, len(peers))

    def tell(r):
        for dz in (1 << r, NZ - (1 << r)):
            pl.semaphore_signal(tsem.at[r], inc=1, device_id=at(dz=dz), device_id_type=MESH)

    def hear(r):
        pl.semaphore_wait(tsem.at[r], 2)

    lo, hi = pl.ds(0, half), pl.ds(half, half)
    up, down = at(dy=1), at(dy=3)

    def r(k):
        all_of(gs.at[pl.ds(1, 3), k], lsem.at[k]).wait()
        remote(gs.at[2, k, lo], rel.at[k, 0], asend, arecv.at[0, k], up).start()
        remote(gs.at[2, k, hi], rel.at[k, 1], asend, arecv.at[0, k], down).start()

    def w(k):
        remote(gs.at[1, k, hi], parts_in.at[k, 0, hi], asend, arecv.at[1, k], up).start()
        remote(gs.at[3, k, lo], parts_in.at[k, 1, lo], asend, arecv.at[1, k], down).start()

    def a2(k):
        remote(rel.at[k], rel.at[k], asend, arecv.at[0, k], up).wait_recv()
        sums[k, 0] = (gs[1, k, 0:half].astype(F32) + rel[k, 0].astype(F32)).astype(BF)
        remote(sums.at[k, 0], parts_in.at[k, 0, lo], asend, arecv.at[1, k], up).start()
        sums[k, 1] = (gs[3, k, half:].astype(F32) + rel[k, 1].astype(F32)).astype(BF)
        remote(sums.at[k, 1], parts_in.at[k, 1, hi], asend, arecv.at[1, k], down).start()

    def exchange_z(s, k):
        for j in FAR_FIRST:
            remote(zsb.at[s, k, j], zrb.at[s, k, j], zsend, zrecv.at[s, k], at(dz=j)).start()

    def arrived_z(s, k):
        every = zrb.at[s, k, pl.ds(1, NZ - 1)]
        remote(every, every, zsend, zrecv.at[s, k], at(dz=1)).wait_recv()

    def exchange_s(s, k):
        for i in (4, 5, 2, 6, 3, 7, 1):
            remote(ssb.at[s, k, i], srb.at[s, k, i], ssend, srecv.at[s, k], at_i(i)).start()

    def arrived_s(s, k):
        every = srb.at[s, k, pl.ds(1, NS - 1)]
        remote(every, every, ssend, srecv.at[s, k], at_i(1)).wait_recv()

    def a3(k):
        remote(parts_in.at[k], parts_in.at[k], asend, arecv.at[1, k], up).wait_recv()
        if k == 0:
            all_of(gs.at[0], lsem.at[n]).wait()
        total = gs[0, k].astype(F32) + parts_in[k, 0].astype(F32) + parts_in[k, 1].astype(F32)
        moved = dot(p1[...], total.astype(BF)).reshape(NZ, 24, C).astype(BF)
        zsb[0, k] = moved
        zrb[0, k, 0] = moved[0]

    def zs(k):
        exchange_z(0, k)

    def b1(k):
        arrived_z(0, k)
        held = zrb[0, k].astype(F32).reshape(rows, C).astype(BF)
        moved = dot(p2[...], held).reshape(NS, 48, C).astype(BF)
        ssb[0, k] = moved
        srb[0, k, 0] = moved[0]
        exchange_s(0, k)

    def b2(k):
        arrived_s(0, k)
        totals = dot(m1[...], srb[0, k].reshape(rows, C))
        cols = slice(k * C, (k + 1) * C)
        new_momentum = momentum_decay * mom_v[:, :, cols].reshape(three, C) + totals
        nm_out[:, :, cols] = new_momentum.reshape(3, experts, C)
        master = mas_v[:, :, cols].reshape(three, C)
        weights = master - step_rate * new_momentum
        parts = []
        for b in range(C // QBLOCK):
            lanes_b = slice(b * QBLOCK, (b + 1) * QBLOCK)
            top = jnp.max(jnp.abs(master[:, lanes_b]), axis=1, keepdims=True)
            scale = (top / range_limit + epsilon).astype(BF).astype(F32)
            quantized = jnp.clip(weights[:, lanes_b] / scale, -range_limit, range_limit).astype(BF)
            parts.append((quantized.astype(F32) * scale).astype(BF))
        restored = parts[0] if len(parts) == 1 else jnp.concatenate(parts, axis=1)
        moved = dot(m2[...], restored).reshape(NS, 48, C).astype(BF)
        ssb[1, k] = moved
        srb[1, k, 0] = moved[0]
        exchange_s(1, k)

    def c1(k):
        arrived_s(1, k)
        moved = dot(p3[...], srb[1, k].reshape(rows, C)).reshape(NZ, 24, C).astype(BF)
        zsb[1, k] = moved
        zrb[1, k, 0] = moved[0]
        exchange_z(1, k)

    lo8, hi8 = pl.ds(0, NZ // 2), pl.ds(NZ // 2, NZ // 2)

    def d1(k):
        arrived_z(1, k)
        remote(zrb.at[1, k, lo8], wb.at[k, 0], dsend, drecv.at[0, k], up).start()
        remote(zrb.at[1, k, hi8], wb.at[k, 1], dsend, drecv.at[0, k], down).start()
        remote(zrb.at[1, k, hi8], wb.at[k, 2], dsend, drecv.at[1, k], up).start()
        remote(zrb.at[1, k, lo8], wb.at[k, 3], dsend, drecv.at[1, k], down).start()

    def multiply(k, held, b):
        weight = held.astype(F32).reshape(rows, C).astype(BF)
        off = pl.multiple_of(lax.rem(y + b, NY) * k_width + k * C, 128)
        out[:, pl.ds(off, C)] = dot(selp[...], weight).astype(BF)

    def halves(k, a, b):
        return jnp.concatenate([wb[k, a], wb[k, b]], axis=0)

    def arrived_d(k, which, first):
        pair = wb.at[k, pl.ds(first, 2)]
        remote(pair, pair, dsend, drecv.at[which, k], up).wait_recv()

    def d2(k):
        arrived_d(k, 0, 0)
        remote(wb.at[k, 0], wb.at[k, 4], dsend, drecv.at[2, k], up).start()
        remote(wb.at[k, 1], wb.at[k, 5], dsend, drecv.at[2, k], down).start()
        multiply(k, zrb[1, k], 0)

    def d3(k):
        arrived_d(k, 1, 2)
        multiply(k, halves(k, 0, 2), 3)
        multiply(k, halves(k, 3, 1), 1)
        arrived_d(k, 2, 4)
        multiply(k, halves(k, 4, 5), 2)

    r(0); w(0); tell(0); r(1); hear(0); tell(1); build_p1()
    a2(0); w(1); r(2); hear(1); tell(2); a2(1); w(2); r(3); a3(0); hear(2); zs(0)
    build_p2(); a2(2); w(3); a3(1); zs(1); build_m1(); a2(3); build_m2(); build_p3(); a3(2)
    cp_mom.wait()
    cp_mas.wait()
    zs(2); a3(3); build_p4(); b1(0); zs(3); select(0); select(1); b1(1); b2(0); b1(2); c1(0); b2(1); select(2); b1(3); b2(2); c1(1); select(3); b2(3); c1(2)
    d1(0); c1(3); d2(0); d1(1); d2(1); d3(0); d1(2); d2(2); d3(1); d1(3); d2(3); d3(2); d3(3)
    remote(gs.at[pl.ds(0, 3)], gs.at[pl.ds(0, 3)], asend, arecv.at[0, 0], up).wait_send()
    sent = zsb.at[:, :, pl.ds(1, NZ - 1)]
    remote(sent, sent, zsend, zrecv.at[0, 0], up).wait_send()
    sent = ssb.at[:, :, pl.ds(1, NS - 1)]
    remote(sent, sent, ssend, srecv.at[0, 0], up).wait_send()
    remote(wb, wb, dsend, drecv.at[0, 0], up).wait_send()


def deliver(nm_in, out_in, nm_out, out, sem):
    copies = [pltpu.make_async_copy(nm_in, nm_out, sem.at[0])]
    part = out.shape[0] // 4
    for q in range(4):
        piece = pl.ds(q * part, part)
        copies.append(pltpu.make_async_copy(out_in.at[piece], out.at[piece], sem.at[q + 1]))
    for cp in copies:
        cp.start()
    for cp in copies:
        cp.wait()


def shards(grads, momentum, master, current_slots, next_slots, live_counts, route_index, activations):
    grad = grads[0, 0]
    rows, width = grad.shape
    columns = momentum.shape[2]
    experts = momentum.shape[1]
    n = CHUNKS
    C = columns // n
    out_rows, hidden = activations.shape[2:]
    half = rows // 2
    hbm = pl.BlockSpec(memory_space=pltpu.MemorySpace.HBM)
    vmem = pl.BlockSpec(memory_space=pltpu.VMEM)

    def buf(*shape):
        return pltpu.VMEM(shape, BF)

    zbuf = buf(2, n, NZ, 24, C)
    sbuf = buf(2, n, NS, 48, C)
    sems = pltpu.SemaphoreType.DMA
    held = lambda a: pltpu.with_memory_space_constraint(a, pltpu.MemorySpace.HBM)
    new_momentum, expert_out = pl.pallas_call(
        functools.partial(kernel, C),
        out_shape=(
            jax.ShapeDtypeStruct(momentum.shape, F32),
            jax.ShapeDtypeStruct((out_rows, width), BF),
        ),
        in_specs=[hbm, hbm, hbm, hbm, hbm, vmem, hbm, hbm],
        out_specs=(vmem, vmem),
        scratch_shapes=[
            buf(NY, n, rows, C),
            pltpu.VMEM(momentum.shape, F32),
            pltpu.VMEM(momentum.shape, F32),
            buf(out_rows, hidden),
            pltpu.VMEM((1, current_slots.shape[0]), jnp.int32),
            pltpu.VMEM((1, current_slots.shape[0]), jnp.int32),
            pltpu.VMEM(route_index.shape[2:], jnp.int32),
            buf(n, 2, half, C), buf(n, 2, half, C), buf(n, 2, rows, C),
            zbuf, zbuf, sbuf, sbuf, buf(n, 6, NZ // 2, 24, C),
            buf(out_rows, hidden),
            buf(rows, rows), buf(rows, rows), buf(rows, rows), buf(rows, rows),
            buf(3 * experts, rows), buf(rows, 3 * experts),
            sems((n + 7,)),
            sems, sems((2, n)), sems, sems((2, n)), sems, sems((2, n)), sems, sems((3, n)),
            pltpu.SemaphoreType.REGULAR((3,)),
        ],
        compiler_params=pltpu.CompilerParams(
            collective_id=0, has_side_effects=True, vmem_limit_bytes=40 * 1024 * 1024
        ),
        name="step",
    )(
        held(grad), held(momentum), held(master), held(current_slots.reshape(1, -1)), held(next_slots.reshape(1, -1)), live_counts,
        held(route_index[0, 0]), held(activations[0, 0]),
    )
    new_momentum, expert_out = pl.pallas_call(
        deliver,
        out_shape=(
            jax.ShapeDtypeStruct(momentum.shape, F32),
            jax.ShapeDtypeStruct((out_rows, width), BF),
        ),
        in_specs=[vmem, vmem],
        out_specs=(hbm, hbm),
        scratch_shapes=[sems((5,))],
        compiler_params=pltpu.CompilerParams(vmem_limit_bytes=1024 * 1024),
        name="deliver",
    )(new_momentum, expert_out)
    return new_momentum, expert_out[None, None]


def solution(mesh):
    in_specs = (
        P("dp", "expert", None, None),
        P("expert", None, "dp"),
        P("expert", None, "dp"),
        P(),
        P(),
        P("dp", "expert"),
        P("dp", "expert", None, None),
        P("dp", "expert", None, None),
    )
    out_specs = (P("expert", None, "dp"), P("dp", "expert", None, None))
    return jax.shard_map(shards, mesh=mesh, in_specs=in_specs, out_specs=out_specs, check_vma=False)
```

```python
import functools

import jax
import jax.numpy as jnp
from jax import lax
from jax.experimental import pallas as pl
from jax.experimental.pallas import tpu as pltpu
from jax.sharding import PartitionSpec as P

MESH = pl.DeviceIdType.MESH
QBLOCK = 128
NY, NX, NZ, NC = 4, 4, 16, 2
NS = NX * NC
CHUNKS = 4
FAR_FIRST = sorted(range(1, NZ), key=lambda j: -min(j, NZ - j))

momentum_decay = 0.9
step_rate = 0.5
epsilon = 1e-06
range_limit = 448.0
BF = jnp.bfloat16
F32 = jnp.float32


def idiv(v, d):
    if d == 3:
        return (v * 171) >> 9
    return idiv(v >> (3 if d == 24 else 4), 3)


def split_jip(r):
    j = idiv(r, 24)
    rem = r - j * 24
    i = idiv(rem, 3)
    return j, i, rem - i * 3


def split_ijp(r):
    i = idiv(r, 48)
    rem = r - i * 48
    j = idiv(rem, 3)
    return i, j, rem - j * 3


def dot(a, b):
    return jnp.dot(a, b, preferred_element_type=F32)


def iota(shape, dim):
    return lax.broadcasted_iota(jnp.int32, shape, dim)


def onehot(cond):
    return jnp.where(cond, 1.0, 0.0).astype(BF)


def kernel(
    C,
    grad, mom, mas, cur_h, nxt_h, live, route_h, act,
    nm_out, out,
    gs, mom_v, mas_v, act_v, cur, nxt, route,
    rel, sums, parts_in, zsb, zrb, ssb, srb, wb,
    selp, p1, p2, p3, p4, m1, m2,
    lsem, asend, arecv, zsend, zrecv, ssend, srecv, dsend, drecv, tsem,
):
    n = CHUNKS
    e = lax.axis_index("expert")
    y = lax.axis_index("dp")
    x, z, c = e // (NZ * NC), (e // NC) % NZ, e % NC
    rows = grad.shape[0]
    half = rows // 2

    def at(dy=0, dx=0, dz=0, dc=0):
        ex = (lax.rem(x + dx, NX) * NZ + lax.rem(z + dz, NZ)) * NC + lax.rem(c + dc, NC)
        return (lax.rem(y + dy, NY), ex)

    def at_i(i):
        return at(dx=i // NC, dc=i % NC)

    def remote(src, dst, ssem, rsem, device):
        return pltpu.make_async_remote_copy(
            src_ref=src, dst_ref=dst, send_sem=ssem, recv_sem=rsem,
            device_id=device, device_id_type=MESH,
        )

    barrier = pltpu.get_barrier_semaphore()
    peers = [at(dz=1), at(dz=NZ - 1)]
    peers += [at_i(i) for i in range(1, NS)]
    peers += [at(dy=1), at(dy=3)]
    for device in peers:
        pl.semaphore_signal(barrier, inc=1, device_id=device, device_id_type=MESH)

    k_width = C * n
    def stage(k, b, sem):
        off = pl.multiple_of(lax.rem(y + b, NY) * k_width + k * C, 128)
        pltpu.make_async_copy(grad.at[:, pl.ds(off, C)], gs.at[b, k], lsem.at[sem]).start()

    for b in (2, 1, 3):
        stage(0, b, 0)
    small = [(act, act_v), (route_h, route), (cur_h, cur), (nxt_h, nxt), (mom, mom_v), (mas, mas_v)]
    small = [pltpu.make_async_copy(src, dst, lsem.at[n + 1 + at_]) for at_, (src, dst) in enumerate(small)]
    cp_act, cp_route, cp_cur, cp_nxt, cp_mom, cp_mas = small

    def stage_rest():
        for k in range(1, n):
            for b in (2, 1, 3):
                stage(k, b, k)
        for k in range(n):
            stage(k, 0, n)
        for cp in (cp_cur, cp_nxt, cp_route, cp_act, cp_mom, cp_mas):
            cp.start()

    def all_of(ref, sem):
        return pltpu.make_async_copy(ref, ref, sem)

    experts = mom_v.shape[1]
    three = 3 * experts

    def build_p1():
        j, i, p = split_jip(iota((rows, 1), 0))
        dest = ((x + (i >> 1)) & 3) * 96 + ((z + j) & 15) * 6 + ((c + (i & 1)) & 1) * 3 + p
        p1[...] = onehot(iota((rows, rows), 1) == dest)

    def build_p2():
        i, j, p = split_ijp(iota((rows, 1), 0))
        p2[...] = onehot(iota((rows, rows), 1) == j * 24 + i * 3 + p)

    def build_p3():
        j, i, p = split_jip(iota((rows, 1), 0))
        p3[...] = onehot(iota((rows, rows), 1) == i * 48 + j * 3 + p)

    def build_m1():
        i, j, p = split_ijp(iota((1, rows), 1))
        slot = (((x - (i >> 1)) & 3) * NZ + ((z - j) & 15)) * NC + ((c + (i & 1)) & 1)
        pick = onehot(iota((128, rows), 0) == slot)
        cp_cur.wait()
        values = jnp.broadcast_to(cur[...].astype(F32), (16, 128)).astype(BF)
        expert_of = dot(values, pick).astype(jnp.int32)[0:1, :]
        m1[...] = onehot(expert_of + experts * p == iota((three, rows), 0))

    def build_m2():
        i, j, p = split_ijp(iota((rows, 1), 0))
        slot = (((x + (i >> 1)) & 3) * NZ + ((z + j) & 15)) * NC + ((c + (i & 1)) & 1)
        pick = onehot(iota((rows, 128), 1) == slot)
        cp_nxt.wait()
        values = jnp.broadcast_to(nxt[...].astype(F32), (128, 128)).T.astype(BF)
        values = jnp.concatenate([values, values], axis=1)[:, 0:three]
        expert_of = dot(pick, values).astype(jnp.int32)
        m2[...] = onehot(expert_of + experts * p == iota((rows, three), 1))

    def build_p4():
        j, i, p = split_jip(iota((1, rows), 1))
        source = ((x - (i >> 1)) & 3) * 96 + ((z - j) & 15) * 6 + ((c + (i & 1)) & 1) * 3 + p
        p4[...] = onehot(iota((rows, rows), 0) == source)
        cp_act.wait()
        cp_route.wait()

    def select(q):
        rb = route.shape[1]
        hit = jnp.where(route[q : q + 1, :] == iota((rb, rb), 0), 1.0, 0.0).astype(F32)
        picked = dot(hit.T.astype(BF), act_v[q * rb : (q + 1) * rb, :])
        alive = iota((rb, 1), 0) + q * rb < live[...]
        picked = jnp.where(alive, picked, 0.0).astype(BF)
        selp[q * rb : (q + 1) * rb, :] = dot(picked, p4[...]).astype(BF)

    pl.semaphore_wait(barrier, len(peers))

    def tell(r):
        for dz in (1 << r, NZ - (1 << r)):
            pl.semaphore_signal(tsem.at[r], inc=1, device_id=at(dz=dz), device_id_type=MESH)

    def hear(r):
        pl.semaphore_wait(tsem.at[r], 2)

    lo, hi = pl.ds(0, half), pl.ds(half, half)
    up, down = at(dy=1), at(dy=3)

    def r(k):
        all_of(gs.at[pl.ds(1, 3), k], lsem.at[k]).wait()
        remote(gs.at[2, k, lo], rel.at[k, 0], asend, arecv.at[0, k], up).start()
        remote(gs.at[2, k, hi], rel.at[k, 1], asend, arecv.at[0, k], down).start()

    def w(k):
        remote(gs.at[1, k, hi], parts_in.at[k, 0, hi], asend, arecv.at[1, k], up).start()
        remote(gs.at[3, k, lo], parts_in.at[k, 1, lo], asend, arecv.at[1, k], down).start()

    def a2(k):
        remote(rel.at[k], rel.at[k], asend, arecv.at[0, k], up).wait_recv()
        sums[k, 0] = (gs[1, k, 0:half].astype(F32) + rel[k, 0].astype(F32)).astype(BF)
        remote(sums.at[k, 0], parts_in.at[k, 0, lo], asend, arecv.at[1, k], up).start()
        sums[k, 1] = (gs[3, k, half:].astype(F32) + rel[k, 1].astype(F32)).astype(BF)
        remote(sums.at[k, 1], parts_in.at[k, 1, hi], asend, arecv.at[1, k], down).start()

    def exchange_z(s, k):
        for j in FAR_FIRST:
            remote(zsb.at[s, k, j], zrb.at[s, k, j], zsend, zrecv.at[s, k], at(dz=j)).start()

    def arrived_z(s, k):
        every = zrb.at[s, k, pl.ds(1, NZ - 1)]
        remote(every, every, zsend, zrecv.at[s, k], at(dz=1)).wait_recv()

    def exchange_s(s, k):
        for i in (4, 5, 2, 6, 3, 7, 1):
            remote(ssb.at[s, k, i], srb.at[s, k, i], ssend, srecv.at[s, k], at_i(i)).start()

    def arrived_s(s, k):
        every = srb.at[s, k, pl.ds(1, NS - 1)]
        remote(every, every, ssend, srecv.at[s, k], at_i(1)).wait_recv()

    def a3(k):
        remote(parts_in.at[k], parts_in.at[k], asend, arecv.at[1, k], up).wait_recv()
        if k == 0:
            all_of(gs.at[0], lsem.at[n]).wait()
        total = gs[0, k].astype(F32) + parts_in[k, 0].astype(F32) + parts_in[k, 1].astype(F32)
        moved = dot(p1[...], total.astype(BF)).reshape(NZ, 24, C).astype(BF)
        zsb[0, k] = moved
        zrb[0, k, 0] = moved[0]

    def zs(k):
        exchange_z(0, k)

    def b1(k):
        arrived_z(0, k)
        held = zrb[0, k].astype(F32).reshape(rows, C).astype(BF)
        moved = dot(p2[...], held).reshape(NS, 48, C).astype(BF)
        ssb[0, k] = moved
        srb[0, k, 0] = moved[0]
        exchange_s(0, k)

    def b2(k):
        arrived_s(0, k)
        totals = dot(m1[...], srb[0, k].reshape(rows, C))
        cols = slice(k * C, (k + 1) * C)
        new_momentum = momentum_decay * mom_v[:, :, cols].reshape(three, C) + totals
        nm_out[:, :, cols] = new_momentum.reshape(3, experts, C)
        master = mas_v[:, :, cols].reshape(three, C)
        weights = master - step_rate * new_momentum
        parts = []
        for b in range(C // QBLOCK):
            lanes_b = slice(b * QBLOCK, (b + 1) * QBLOCK)
            top = jnp.max(jnp.abs(master[:, lanes_b]), axis=1, keepdims=True)
            scale = (top / range_limit + epsilon).astype(BF).astype(F32)
            quantized = jnp.clip(weights[:, lanes_b] / scale, -range_limit, range_limit).astype(BF)
            parts.append((quantized.astype(F32) * scale).astype(BF))
        restored = parts[0] if len(parts) == 1 else jnp.concatenate(parts, axis=1)
        moved = dot(m2[...], restored).reshape(NS, 48, C).astype(BF)
        ssb[1, k] = moved
        srb[1, k, 0] = moved[0]
        exchange_s(1, k)

    def c1(k):
        arrived_s(1, k)
        moved = dot(p3[...], srb[1, k].reshape(rows, C)).reshape(NZ, 24, C).astype(BF)
        zsb[1, k] = moved
        zrb[1, k, 0] = moved[0]
        exchange_z(1, k)

    lo8, hi8 = pl.ds(0, NZ // 2), pl.ds(NZ // 2, NZ // 2)

    def d1(k):
        arrived_z(1, k)
        remote(zrb.at[1, k, lo8], wb.at[k, 0], dsend, drecv.at[0, k], up).start()
        remote(zrb.at[1, k, hi8], wb.at[k, 1], dsend, drecv.at[0, k], down).start()
        remote(zrb.at[1, k, hi8], wb.at[k, 2], dsend, drecv.at[1, k], up).start()
        remote(zrb.at[1, k, lo8], wb.at[k, 3], dsend, drecv.at[1, k], down).start()

    def multiply(k, held, b):
        weight = held.astype(F32).reshape(rows, C).astype(BF)
        off = pl.multiple_of(lax.rem(y + b, NY) * k_width + k * C, 128)
        out[:, pl.ds(off, C)] = dot(selp[...], weight).astype(BF)

    def halves(k, a, b):
        return jnp.concatenate([wb[k, a], wb[k, b]], axis=0)

    def arrived_d(k, which, first):
        pair = wb.at[k, pl.ds(first, 2)]
        remote(pair, pair, dsend, drecv.at[which, k], up).wait_recv()

    def d2(k):
        arrived_d(k, 0, 0)
        remote(wb.at[k, 0], wb.at[k, 4], dsend, drecv.at[2, k], up).start()
        remote(wb.at[k, 1], wb.at[k, 5], dsend, drecv.at[2, k], down).start()
        multiply(k, zrb[1, k], 0)

    def d3(k):
        arrived_d(k, 1, 2)
        multiply(k, halves(k, 0, 2), 3)
        multiply(k, halves(k, 3, 1), 1)
        arrived_d(k, 2, 4)
        multiply(k, halves(k, 4, 5), 2)

    r(0); w(0); tell(0); stage_rest(); r(1); hear(0); tell(1); build_p1()
    a2(0); w(1); r(2); hear(1); tell(2); a2(1); w(2); r(3); a3(0); hear(2); zs(0)
    build_p2(); a2(2); w(3); a3(1); zs(1); build_m1(); a2(3); build_m2(); build_p3(); a3(2)
    cp_mom.wait()
    cp_mas.wait()
    zs(2); a3(3); build_p4(); b1(0); zs(3); select(0); select(1); b1(1); b2(0); b1(2); c1(0); b2(1); select(2); b1(3); b2(2); c1(1); select(3); b2(3); c1(2)
    d1(0); c1(3); d2(0); d1(1); d2(1); d1(2); d3(0); d2(2); d1(3); d3(1); d2(3); d3(2); d3(3)
    remote(gs.at[pl.ds(0, 3)], gs.at[pl.ds(0, 3)], asend, arecv.at[0, 0], up).wait_send()
    sent = zsb.at[:, :, pl.ds(1, NZ - 1)]
    remote(sent, sent, zsend, zrecv.at[0, 0], up).wait_send()
    sent = ssb.at[:, :, pl.ds(1, NS - 1)]
    remote(sent, sent, ssend, srecv.at[0, 0], up).wait_send()
    remote(wb, wb, dsend, drecv.at[0, 0], up).wait_send()


def deliver(nm_in, out_in, nm_out, out, sem):
    copies = [pltpu.make_async_copy(out_in, out, sem.at[0]), pltpu.make_async_copy(nm_in, nm_out, sem.at[1])]
    for cp in copies:
        cp.start()
    for cp in copies:
        cp.wait()


def shards(grads, momentum, master, current_slots, next_slots, live_counts, route_index, activations):
    grad = grads[0, 0]
    rows, width = grad.shape
    columns = momentum.shape[2]
    experts = momentum.shape[1]
    n = CHUNKS
    C = columns // n
    out_rows, hidden = activations.shape[2:]
    half = rows // 2
    hbm = pl.BlockSpec(memory_space=pltpu.MemorySpace.HBM)
    vmem = pl.BlockSpec(memory_space=pltpu.VMEM)

    def buf(*shape):
        return pltpu.VMEM(shape, BF)

    zbuf = buf(2, n, NZ, 24, C)
    sbuf = buf(2, n, NS, 48, C)
    sems = pltpu.SemaphoreType.DMA
    held = lambda a: pltpu.with_memory_space_constraint(a, pltpu.MemorySpace.HBM)
    new_momentum, expert_out = pl.pallas_call(
        functools.partial(kernel, C),
        out_shape=(
            jax.ShapeDtypeStruct(momentum.shape, F32),
            jax.ShapeDtypeStruct((out_rows, width), BF),
        ),
        in_specs=[hbm, hbm, hbm, hbm, hbm, vmem, hbm, hbm],
        out_specs=(vmem, vmem),
        scratch_shapes=[
            buf(NY, n, rows, C),
            pltpu.VMEM(momentum.shape, F32),
            pltpu.VMEM(momentum.shape, F32),
            buf(out_rows, hidden),
            pltpu.VMEM((1, current_slots.shape[0]), jnp.int32),
            pltpu.VMEM((1, current_slots.shape[0]), jnp.int32),
            pltpu.VMEM(route_index.shape[2:], jnp.int32),
            buf(n, 2, half, C), buf(n, 2, half, C), buf(n, 2, rows, C),
            zbuf, zbuf, sbuf, sbuf, buf(n, 6, NZ // 2, 24, C),
            buf(out_rows, hidden),
            buf(rows, rows), buf(rows, rows), buf(rows, rows), buf(rows, rows),
            buf(3 * experts, rows), buf(rows, 3 * experts),
            sems((n + 7,)),
            sems, sems((2, n)), sems, sems((2, n)), sems, sems((2, n)), sems, sems((3, n)),
            pltpu.SemaphoreType.REGULAR((3,)),
        ],
        compiler_params=pltpu.CompilerParams(
            collective_id=0, has_side_effects=True, vmem_limit_bytes=40 * 1024 * 1024
        ),
        name="step",
    )(
        held(grad), held(momentum), held(master), held(current_slots.reshape(1, -1)), held(next_slots.reshape(1, -1)), live_counts,
        held(route_index[0, 0]), held(activations[0, 0]),
    )
    new_momentum, expert_out = pl.pallas_call(
        deliver,
        out_shape=(
            jax.ShapeDtypeStruct(momentum.shape, F32),
            jax.ShapeDtypeStruct((out_rows, width), BF),
        ),
        in_specs=[vmem, vmem],
        out_specs=(hbm, hbm),
        scratch_shapes=[sems((2,))],
        compiler_params=pltpu.CompilerParams(vmem_limit_bytes=1024 * 1024),
        name="deliver",
    )(new_momentum, expert_out)
    return new_momentum, expert_out[None, None]


def solution(mesh):
    in_specs = (
        P("dp", "expert", None, None),
        P("expert", None, "dp"),
        P("expert", None, "dp"),
        P(),
        P(),
        P("dp", "expert"),
        P("dp", "expert", None, None),
        P("dp", "expert", None, None),
    )
    out_specs = (P("expert", None, "dp"), P("dp", "expert", None, None))
    return jax.shard_map(shards, mesh=mesh, in_specs=in_specs, out_specs=out_specs, check_vma=False)
```

```python
import functools

import jax
import jax.numpy as jnp
from jax import lax
from jax.experimental import pallas as pl
from jax.experimental.pallas import tpu as pltpu
from jax.sharding import PartitionSpec as P

MESH = pl.DeviceIdType.MESH
QBLOCK = 128
NY, NX, NZ, NC = 4, 4, 16, 2
NS = NX * NC
CHUNKS = 4
FAR_FIRST = sorted(range(1, NZ), key=lambda j: -min(j, NZ - j))

momentum_decay = 0.9
step_rate = 0.5
epsilon = 1e-06
range_limit = 448.0
BF = jnp.bfloat16
F32 = jnp.float32


def idiv(v, d):
    if d == 3:
        return (v * 171) >> 9
    return idiv(v >> (3 if d == 24 else 4), 3)


def split_jip(r):
    j = idiv(r, 24)
    rem = r - j * 24
    i = idiv(rem, 3)
    return j, i, rem - i * 3


def split_ijp(r):
    i = idiv(r, 48)
    rem = r - i * 48
    j = idiv(rem, 3)
    return i, j, rem - j * 3


def dot(a, b):
    return jnp.dot(a, b, preferred_element_type=F32)


def iota(shape, dim):
    return lax.broadcasted_iota(jnp.int32, shape, dim)


def onehot(cond):
    return jnp.where(cond, 1.0, 0.0).astype(BF)


def kernel(
    C,
    grad, mom, mas, cur_h, nxt_h, live, route_h, act,
    nm_out, out,
    gs, mom_v, mas_v, act_v, cur, nxt, route,
    rel, sums, parts_in, zsb, zrb, ssb, srb, wb,
    selp, p1, p2, p3, p4, m1, m2,
    lsem, asend, arecv, zsend, zrecv, ssend, srecv, dsend, drecv, tsem,
):
    n = CHUNKS
    e = lax.axis_index("expert")
    y = lax.axis_index("dp")
    x, z, c = e // (NZ * NC), (e // NC) % NZ, e % NC
    rows = grad.shape[0]
    half = rows // 2

    def at(dy=0, dx=0, dz=0, dc=0):
        ex = (lax.rem(x + dx, NX) * NZ + lax.rem(z + dz, NZ)) * NC + lax.rem(c + dc, NC)
        return (lax.rem(y + dy, NY), ex)

    def at_i(i):
        return at(dx=i // NC, dc=i % NC)

    def remote(src, dst, ssem, rsem, device):
        return pltpu.make_async_remote_copy(
            src_ref=src, dst_ref=dst, send_sem=ssem, recv_sem=rsem,
            device_id=device, device_id_type=MESH,
        )

    barrier = pltpu.get_barrier_semaphore()
    peers = [at(dz=1), at(dz=NZ - 1)]
    peers += [at_i(i) for i in range(1, NS)]
    peers += [at(dy=1), at(dy=3)]
    for device in peers:
        pl.semaphore_signal(barrier, inc=1, device_id=device, device_id_type=MESH)

    k_width = C * n
    def stage(k, b, sem):
        off = pl.multiple_of(lax.rem(y + b, NY) * k_width + k * C, 128)
        pltpu.make_async_copy(grad.at[:, pl.ds(off, C)], gs.at[b, k], lsem.at[sem]).start()

    for b in (2, 1, 3):
        stage(0, b, 0)
    small = [(act, act_v), (route_h, route), (cur_h, cur), (nxt_h, nxt), (mom, mom_v), (mas, mas_v)]
    small = [pltpu.make_async_copy(src, dst, lsem.at[n + 1 + at_]) for at_, (src, dst) in enumerate(small)]
    cp_act, cp_route, cp_cur, cp_nxt, cp_mom, cp_mas = small

    def stage_rest():
        for k in range(1, n):
            for b in (2, 1, 3):
                stage(k, b, k)
        for k in range(n):
            stage(k, 0, n)
        for cp in (cp_cur, cp_nxt, cp_route, cp_act, cp_mom, cp_mas):
            cp.start()

    def all_of(ref, sem):
        return pltpu.make_async_copy(ref, ref, sem)

    experts = mom_v.shape[1]
    three = 3 * experts

    def build_p1():
        j, i, p = split_jip(iota((rows, 1), 0))
        dest = ((x + (i >> 1)) & 3) * 96 + ((z + j) & 15) * 6 + ((c + (i & 1)) & 1) * 3 + p
        p1[...] = onehot(iota((rows, rows), 1) == dest)

    def build_p2():
        i, j, p = split_ijp(iota((rows, 1), 0))
        p2[...] = onehot(iota((rows, rows), 1) == j * 24 + i * 3 + p)

    def build_p3():
        j, i, p = split_jip(iota((rows, 1), 0))
        p3[...] = onehot(iota((rows, rows), 1) == i * 48 + j * 3 + p)

    def build_m1():
        i, j, p = split_ijp(iota((1, rows), 1))
        slot = (((x - (i >> 1)) & 3) * NZ + ((z - j) & 15)) * NC + ((c + (i & 1)) & 1)
        pick = onehot(iota((128, rows), 0) == slot)
        cp_cur.wait()
        values = jnp.broadcast_to(cur[...].astype(F32), (16, 128)).astype(BF)
        expert_of = dot(values, pick).astype(jnp.int32)[0:1, :]
        m1[...] = onehot(expert_of + experts * p == iota((three, rows), 0))

    def build_m2():
        i, j, p = split_ijp(iota((rows, 1), 0))
        slot = (((x + (i >> 1)) & 3) * NZ + ((z + j) & 15)) * NC + ((c + (i & 1)) & 1)
        pick = onehot(iota((rows, 128), 1) == slot)
        cp_nxt.wait()
        values = jnp.broadcast_to(nxt[...].astype(F32), (128, 128)).T.astype(BF)
        values = jnp.concatenate([values, values], axis=1)[:, 0:three]
        expert_of = dot(pick, values).astype(jnp.int32)
        m2[...] = onehot(expert_of + experts * p == iota((rows, three), 1))

    def build_p4():
        j, i, p = split_jip(iota((1, rows), 1))
        source = ((x - (i >> 1)) & 3) * 96 + ((z - j) & 15) * 6 + ((c + (i & 1)) & 1) * 3 + p
        p4[...] = onehot(iota((rows, rows), 0) == source)
        cp_act.wait()
        cp_route.wait()

    def select(q):
        rb = route.shape[1]
        hit = jnp.where(route[q : q + 1, :] == iota((rb, rb), 0), 1.0, 0.0).astype(F32)
        picked = dot(hit.T.astype(BF), act_v[q * rb : (q + 1) * rb, :])
        alive = iota((rb, 1), 0) + q * rb < live[...]
        picked = jnp.where(alive, picked, 0.0).astype(BF)
        selp[q * rb : (q + 1) * rb, :] = dot(picked, p4[...]).astype(BF)

    pl.semaphore_wait(barrier, len(peers))

    def tell(r):
        for dz in (1 << r, NZ - (1 << r)):
            pl.semaphore_signal(tsem.at[r], inc=1, device_id=at(dz=dz), device_id_type=MESH)

    def hear(r):
        pl.semaphore_wait(tsem.at[r], 2)

    lo, hi = pl.ds(0, half), pl.ds(half, half)
    up, down = at(dy=1), at(dy=3)

    def r(k):
        all_of(gs.at[pl.ds(1, 3), k], lsem.at[k]).wait()
        remote(gs.at[2, k, lo], rel.at[k, 0], asend, arecv.at[0, k], up).start()
        remote(gs.at[2, k, hi], rel.at[k, 1], asend, arecv.at[0, k], down).start()

    def w(k):
        remote(gs.at[1, k, hi], parts_in.at[k, 0, hi], asend, arecv.at[1, k], up).start()
        remote(gs.at[3, k, lo], parts_in.at[k, 1, lo], asend, arecv.at[1, k], down).start()

    def a2(k):
        remote(rel.at[k], rel.at[k], asend, arecv.at[0, k], up).wait_recv()
        sums[k, 0] = (gs[1, k, 0:half].astype(F32) + rel[k, 0].astype(F32)).astype(BF)
        remote(sums.at[k, 0], parts_in.at[k, 0, lo], asend, arecv.at[1, k], up).start()
        sums[k, 1] = (gs[3, k, half:].astype(F32) + rel[k, 1].astype(F32)).astype(BF)
        remote(sums.at[k, 1], parts_in.at[k, 1, hi], asend, arecv.at[1, k], down).start()

    def exchange_z(s, k):
        for j in FAR_FIRST:
            remote(zsb.at[s, k, j], zrb.at[s, k, j], zsend, zrecv.at[s, k], at(dz=j)).start()

    def arrived_z(s, k):
        every = zrb.at[s, k, pl.ds(1, NZ - 1)]
        remote(every, every, zsend, zrecv.at[s, k], at(dz=1)).wait_recv()

    def exchange_s(s, k):
        for i in (4, 5, 2, 6, 3, 7, 1):
            remote(ssb.at[s, k, i], srb.at[s, k, i], ssend, srecv.at[s, k], at_i(i)).start()

    def arrived_s(s, k):
        every = srb.at[s, k, pl.ds(1, NS - 1)]
        remote(every, every, ssend, srecv.at[s, k], at_i(1)).wait_recv()

    def a3(k):
        remote(parts_in.at[k], parts_in.at[k], asend, arecv.at[1, k], up).wait_recv()
        if k == 0:
            all_of(gs.at[0], lsem.at[n]).wait()
        total = gs[0, k].astype(F32) + parts_in[k, 0].astype(F32) + parts_in[k, 1].astype(F32)
        moved = dot(p1[...], total.astype(BF)).reshape(NZ, 24, C).astype(BF)
        zsb[0, k] = moved
        zrb[0, k, 0] = moved[0]

    def zs(k):
        exchange_z(0, k)

    def b1(k):
        arrived_z(0, k)
        held = zrb[0, k].astype(F32).reshape(rows, C).astype(BF)
        moved = dot(p2[...], held).reshape(NS, 48, C).astype(BF)
        ssb[0, k] = moved
        srb[0, k, 0] = moved[0]
        exchange_s(0, k)

    def b2(k):
        arrived_s(0, k)
        totals = dot(m1[...], srb[0, k].reshape(rows, C))
        cols = slice(k * C, (k + 1) * C)
        new_momentum = momentum_decay * mom_v[:, :, cols].reshape(three, C) + totals
        nm_out[:, :, cols] = new_momentum.reshape(3, experts, C)
        master = mas_v[:, :, cols].reshape(three, C)
        weights = master - step_rate * new_momentum
        parts = []
        for b in range(C // QBLOCK):
            lanes_b = slice(b * QBLOCK, (b + 1) * QBLOCK)
            top = jnp.max(jnp.abs(master[:, lanes_b]), axis=1, keepdims=True)
            scale = (top / range_limit + epsilon).astype(BF).astype(F32)
            quantized = jnp.clip(weights[:, lanes_b] / scale, -range_limit, range_limit).astype(BF)
            parts.append((quantized.astype(F32) * scale).astype(BF))
        restored = parts[0] if len(parts) == 1 else jnp.concatenate(parts, axis=1)
        moved = dot(m2[...], restored).reshape(NS, 48, C).astype(BF)
        ssb[1, k] = moved
        srb[1, k, 0] = moved[0]
        exchange_s(1, k)

    def c1(k):
        arrived_s(1, k)
        moved = dot(p3[...], srb[1, k].reshape(rows, C)).reshape(NZ, 24, C).astype(BF)
        zsb[1, k] = moved
        zrb[1, k, 0] = moved[0]
        exchange_z(1, k)

    lo8, hi8 = pl.ds(0, NZ // 2), pl.ds(NZ // 2, NZ // 2)

    def d1(k):
        arrived_z(1, k)
        remote(zrb.at[1, k, lo8], wb.at[k, 0], dsend, drecv.at[0, k], up).start()
        remote(zrb.at[1, k, hi8], wb.at[k, 1], dsend, drecv.at[0, k], down).start()
        remote(zrb.at[1, k, hi8], wb.at[k, 2], dsend, drecv.at[1, k], up).start()
        remote(zrb.at[1, k, lo8], wb.at[k, 3], dsend, drecv.at[1, k], down).start()

    def multiply(k, held, b):
        weight = held.astype(F32).reshape(rows, C).astype(BF)
        off = pl.multiple_of(lax.rem(y + b, NY) * k_width + k * C, 128)
        out[:, pl.ds(off, C)] = dot(selp[...], weight).astype(BF)

    def halves(k, a, b):
        return jnp.concatenate([wb[k, a], wb[k, b]], axis=0)

    def arrived_d(k, which, first):
        pair = wb.at[k, pl.ds(first, 2)]
        remote(pair, pair, dsend, drecv.at[which, k], up).wait_recv()

    def d2(k):
        arrived_d(k, 0, 0)
        remote(wb.at[k, 0], wb.at[k, 4], dsend, drecv.at[2, k], up).start()
        remote(wb.at[k, 1], wb.at[k, 5], dsend, drecv.at[2, k], down).start()
        multiply(k, zrb[1, k], 0)

    def d3(k):
        arrived_d(k, 1, 2)
        multiply(k, halves(k, 0, 2), 3)
        multiply(k, halves(k, 3, 1), 1)
        arrived_d(k, 2, 4)
        multiply(k, halves(k, 4, 5), 2)

    r(0); w(0); tell(0); stage_rest(); r(1); w(1); hear(0); tell(1); build_p1()
    a2(0); r(2); w(2); hear(1); tell(2); a2(1); r(3); w(3); a3(0); hear(2); zs(0)
    a2(2); a3(1); zs(1); a2(3); build_p2(); a3(2); zs(2); build_m1(); build_p3(); a3(3); zs(3); b1(0)
    build_m2(); build_p4(); select(0)
    cp_mom.wait()
    cp_mas.wait()
    b1(1); b2(0); b1(2); select(1); c1(0); b2(1); b1(3); select(2); b2(2); c1(1); select(3); b2(3); c1(2)
    d1(0); c1(3); d2(0); d1(1); d2(1); d1(2); d3(0); d2(2); d1(3); d3(1); d2(3); d3(2); d3(3)
    remote(gs.at[pl.ds(0, 3)], gs.at[pl.ds(0, 3)], asend, arecv.at[0, 0], up).wait_send()
    sent = zsb.at[:, :, pl.ds(1, NZ - 1)]
    remote(sent, sent, zsend, zrecv.at[0, 0], up).wait_send()
    sent = ssb.at[:, :, pl.ds(1, NS - 1)]
    remote(sent, sent, ssend, srecv.at[0, 0], up).wait_send()
    remote(wb, wb, dsend, drecv.at[0, 0], up).wait_send()


def deliver(nm_in, out_in, nm_out, out, sem):
    copies = [pltpu.make_async_copy(out_in, out, sem.at[0]), pltpu.make_async_copy(nm_in, nm_out, sem.at[1])]
    for cp in copies:
        cp.start()
    for cp in copies:
        cp.wait()


def shards(grads, momentum, master, current_slots, next_slots, live_counts, route_index, activations):
    grad = grads[0, 0]
    rows, width = grad.shape
    columns = momentum.shape[2]
    experts = momentum.shape[1]
    n = CHUNKS
    C = columns // n
    out_rows, hidden = activations.shape[2:]
    half = rows // 2
    hbm = pl.BlockSpec(memory_space=pltpu.MemorySpace.HBM)
    vmem = pl.BlockSpec(memory_space=pltpu.VMEM)

    def buf(*shape):
        return pltpu.VMEM(shape, BF)

    zbuf = buf(2, n, NZ, 24, C)
    sbuf = buf(2, n, NS, 48, C)
    sems = pltpu.SemaphoreType.DMA
    held = lambda a: pltpu.with_memory_space_constraint(a, pltpu.MemorySpace.HBM)
    new_momentum, expert_out = pl.pallas_call(
        functools.partial(kernel, C),
        out_shape=(
            jax.ShapeDtypeStruct(momentum.shape, F32),
            jax.ShapeDtypeStruct((out_rows, width), BF),
        ),
        in_specs=[hbm, hbm, hbm, hbm, hbm, vmem, hbm, hbm],
        out_specs=(vmem, vmem),
        scratch_shapes=[
            buf(NY, n, rows, C),
            pltpu.VMEM(momentum.shape, F32),
            pltpu.VMEM(momentum.shape, F32),
            buf(out_rows, hidden),
            pltpu.VMEM((1, current_slots.shape[0]), jnp.int32),
            pltpu.VMEM((1, current_slots.shape[0]), jnp.int32),
            pltpu.VMEM(route_index.shape[2:], jnp.int32),
            buf(n, 2, half, C), buf(n, 2, half, C), buf(n, 2, rows, C),
            zbuf, zbuf, sbuf, sbuf, buf(n, 6, NZ // 2, 24, C),
            buf(out_rows, hidden),
            buf(rows, rows), buf(rows, rows), buf(rows, rows), buf(rows, rows),
            buf(3 * experts, rows), buf(rows, 3 * experts),
            sems((n + 7,)),
            sems, sems((2, n)), sems, sems((2, n)), sems, sems((2, n)), sems, sems((3, n)),
            pltpu.SemaphoreType.REGULAR((3,)),
        ],
        compiler_params=pltpu.CompilerParams(
            collective_id=0, has_side_effects=True, vmem_limit_bytes=40 * 1024 * 1024
        ),
        name="step",
    )(
        held(grad), held(momentum), held(master), held(current_slots.reshape(1, -1)), held(next_slots.reshape(1, -1)), live_counts,
        held(route_index[0, 0]), held(activations[0, 0]),
    )
    new_momentum, expert_out = pl.pallas_call(
        deliver,
        out_shape=(
            jax.ShapeDtypeStruct(momentum.shape, F32),
            jax.ShapeDtypeStruct((out_rows, width), BF),
        ),
        in_specs=[vmem, vmem],
        out_specs=(hbm, hbm),
        scratch_shapes=[sems((2,))],
        compiler_params=pltpu.CompilerParams(vmem_limit_bytes=1024 * 1024),
        name="deliver",
    )(new_momentum, expert_out)
    return new_momentum, expert_out[None, None]


def solution(mesh):
    in_specs = (
        P("dp", "expert", None, None),
        P("expert", None, "dp"),
        P("expert", None, "dp"),
        P(),
        P(),
        P("dp", "expert"),
        P("dp", "expert", None, None),
        P("dp", "expert", None, None),
    )
    out_specs = (P("expert", None, "dp"), P("dp", "expert", None, None))
    return jax.shard_map(shards, mesh=mesh, in_specs=in_specs, out_specs=out_specs, check_vma=False)
```
